32 devices in a mesh: groups: 2 (over y), row: 4 (over z), col: 2 (over x), sub: 2 (over core).
Axes of the slice: x: 2, y: 2, z: 4, core: 2. Of those that a mesh axis runs over, the one named last changes fastest.
Arguments:
- query_acts: bfloat16 [64, 128, 4096], P(('groups', 'col', 'sub'), None, 'row'), parts along dimension 0, may hold values from -6 to 6
- query_grads: bfloat16 [64, 128, 4096], P(('groups', 'col', 'sub'), None, 'row'), parts along dimension 0, may hold values from -0.5390625 to 0.5390625
- proj_in: bfloat16 [4096, 128], P('row'), may hold values from -0.09375 to 0.09375
- proj_out: bfloat16 [4096, 128], P('row'), may hold values from -0.09375 to 0.09375
- inverse_gram: float32 [16384, 16384], P('row', ('col', 'sub')), may hold values from -0.01 to 2.01, as said below
- store_slab: bfloat16 [2048, 16384], P(('groups', 'col'), ('row', 'sub')), parts along dimension 0, may hold values from -0.046875 to 0.046875
Outputs:
- scores: float32 [64, 1024], P('groups', 'col'), parts along dimension 0
The draws below stay inside these ranges and needn't reach their ends.
There are 2 independent parts, one for each index of `groups`. The reference program is written for one: setup_inputs(seed, part) draws one part's arguments, and reference() takes and returns one part's arrays. A program takes and returns all parts, laid end to end along the dimension named above; an argument that names none is the same for every part. Nothing has to cross between parts.
Inputs may be any that keep to these rules, and one draw needn't show every extreme that they name: inverse_gram is symmetric.
All inputs are finite; a program needn't handle non-finite values.
Results may differ from the reference program's by a relative error of at most 0.0029.
Values may be sent and summed in bfloat16 or wider, within the bound.
A program may use at most 128 MiB of HBM per device.

```python
import math
import jax
import jax.numpy as jnp
from jax import lax

D = 4096
K_IN = 128
K_OUT = 128
Q = 32
S = 128
F = 16384
E = 1024


def draw_inverse_gram(key, part):
    feature_count = K_IN * K_OUT
    first_key, second_key = jax.random.split(jax.random.fold_in(key, 11))
    noise = jax.random.uniform(first_key, (feature_count, feature_count), jnp.float32, -1.0, 1.0)
    symmetric = (noise + noise.T) * 0.005
    diagonal = jnp.exp(jax.random.uniform(second_key, (feature_count,), jnp.float32, math.log(0.5), math.log(2.0)))
    positions = jnp.arange(feature_count)
    return symmetric.at[positions, positions].add(diagonal)


def block_levels(own_key, extent, cuts, low, top_value):
    gain = 1.0
    for position, shards_of in cuts:
        steps = jax.random.uniform(jax.random.fold_in(jax.random.fold_in(own_key, 6), position), (shards_of,), jnp.float32, low / len(cuts), top_value / len(cuts))
        gain = gain * jnp.repeat(jnp.exp(steps), extent[position] // shards_of).reshape((-1,) + (1,) * (len(extent) - 1 - position))
    return gain


def bell_draw(key, dims, deviation, reach, pieces=(), kind=jnp.bfloat16):
    gain = block_levels(key, dims, pieces, -0.22, 0.18) if pieces else 1.0
    entries = jax.random.normal(key, dims, jnp.float32) * deviation * gain
    return jnp.minimum(jnp.maximum(entries, -reach), reach).astype(kind)


def setup_inputs(seed: int = 0, part: int = 0) -> dict:
    key_of = jax.random.split(jax.random.key(seed), 7)
    part_splits = jax.random.split(jax.random.fold_in(key_of[6], part), 7)
    return {
        "query_acts": bell_draw(part_splits[0], (Q, S, D), 1.0, 6.0, ((0, 4), (2, 4))),
        "query_grads": bell_draw(part_splits[1], (Q, S, D), 0.09, 0.5390625, ((0, 4), (2, 4))),
        "proj_in": bell_draw(key_of[2], (D, K_IN), D ** -0.5, 0.09375, ((0, 4),)),
        "proj_out": bell_draw(key_of[3], (D, K_OUT), D ** -0.5, 0.09375, ((0, 4),)),
        "inverse_gram": draw_inverse_gram(jax.random.fold_in(key_of[6], 71), part),
        "store_slab": bell_draw(part_splits[5], (E, F), F ** -0.5, 0.046875, ((0, 2), (1, 8))),
    }


def reference(query_acts, query_grads, proj_in, proj_out, inverse_gram, store_slab):
    act_proj = jnp.einsum("qtd,dk->qtk", query_acts.astype(jnp.float32), proj_in.astype(jnp.float32), precision=lax.Precision.HIGHEST)
    grad_proj = jnp.einsum("qtd,dk->qtk", query_grads.astype(jnp.float32), proj_out.astype(jnp.float32), precision=lax.Precision.HIGHEST)
    kron_feats = jnp.einsum("qta,qtb->qab", act_proj, grad_proj, precision=lax.Precision.HIGHEST)
    kron_feats = kron_feats.reshape(kron_feats.shape[0], -1)
    precond = jnp.dot(kron_feats, inverse_gram, precision=lax.Precision.HIGHEST)
    precond_b = precond.astype(jnp.bfloat16)
    return jnp.dot(precond_b, store_slab.T, preferred_element_type=jnp.float32)
```

```python
import functools
import math

import jax
import jax.numpy as jnp
from jax import lax
from jax.experimental import pallas as pl
from jax.experimental.pallas import tpu as pltpu
from jax.sharding import PartitionSpec as P

F32, BF16 = jnp.float32, jnp.bfloat16
LAG = 3
ACT_MAX, GRAD_MAX, PROJ_MAX, GRAM_MAX = 6.0, 0.5390625, 0.09375, 2.01


def split(x):
    hi = x.astype(BF16)
    return hi, (x - hi.astype(F32)).astype(BF16)


def scale_of(p, bound):
    return 2.0 ** math.floor(126 / p - math.log2(bound))


def encode(x, p, scale):
    z = x * scale
    if p == 2:
        y = z * jnp.abs(z)
    elif p == 3:
        y = z * z * z
    else:
        y = (z * z) * (z * jnp.abs(z))
    return y.astype(BF16)


def decode(y, p, scale):
    y = y.astype(F32)
    m = jnp.abs(y)
    if p == 2:
        v = m * lax.rsqrt(m) * (1.0 / scale)
    elif p == 3:
        v = jnp.exp2(jnp.log2(m) * (1.0 / 3.0)) * (1.0 / scale)
    else:
        v = lax.rsqrt(lax.rsqrt(m)) * (1.0 / scale)
    return jnp.where(y > 0, v, jnp.where(y < 0, -v, 0.0))


def kernel(groups, rows, cols, subs, acts_h, grads_h, pin_h, pout_h, gram_h, store_h, out,
           acts, grads, pin, pout, gram, store, part, send, recv, fsend, fbuf, feats, ft,
           pre, sub_in, tot, ysend, yin, xsend, xin,
           own, own_s, half_in, half_all, half_out,
           p_sem, in_sem, gram_sem, store_sem, rs_send, rs_recv, fx_send, fx_recv, fx_local, fz_send, fz_recv,
           ps_send, ps_recv, py_send, py_recv, pc_send, pc_recv, ss_sem, sz_send, sz_recv, sf_sem):
    g, r, c, s = (lax.axis_index(n) for n in ("groups", "row", "col", "sub"))
    queries, tokens, depth = acts.shape
    planes = cols * subs
    slices = groups * planes
    me = c * subs + s
    spot = me * groups + g
    source = g * planes + me
    aw, kout = feats.shape[2], feats.shape[3]
    blocks, mb, kw = gram.shape
    per = blocks // subs
    other = lax.rem(s + 1, subs)
    nq = planes * queries
    homes = -(-queries // rows)
    act_bound = rows * depth * ACT_MAX * PROJ_MAX
    grad_bound = rows * depth * GRAD_MAX * PROJ_MAX
    feat_bound = tokens * act_bound * grad_bound
    ps = scale_of(4, max(act_bound, grad_bound))
    fs = scale_of(3, feat_bound)
    gs = scale_of(2, feat_bound * GRAM_MAX * gram_h.shape[1] * planes)

    def dev(group, row, col, sub):
        return {"groups": group, "row": row, "col": col, "sub": sub}

    def remote(src, dst, snd, rcv, group, row, col, sub):
        return pltpu.make_async_remote_copy(
            src_ref=src, dst_ref=dst, send_sem=snd, recv_sem=rcv,
            device_id=dev(group, row, col, sub), device_id_type=pl.DeviceIdType.MESH)

    def at_spot(o):
        plane = o // groups
        return lax.rem(o, groups), r, plane // subs, lax.rem(plane, subs)

    def first(row):
        return (row * queries + rows - 1) // rows

    lo, hi = first(r), first(r + 1)
    lower, upper = jnp.maximum(r - 1, 0), jnp.minimum(r + 1, rows - 1)

    loads = [pltpu.make_async_copy(pin_h, pin, p_sem.at[0]), pltpu.make_async_copy(pout_h, pout, p_sem.at[1])]
    for l in loads:
        l.start()

    def pick(i):
        return jnp.where(2 * r < rows, queries - 1 - i, i)

    def load(i):
        q = pick(i)
        return (pltpu.make_async_copy(acts_h.at[q], acts.at[q], in_sem.at[q, 0]),
                pltpu.make_async_copy(grads_h.at[q], grads.at[q], in_sem.at[q, 1]))

    for i in range(queries):
        for l in load(i):
            l.start()

    def gram_copy(n):
        i = lax.rem(other * per + n, blocks)
        return pltpu.make_async_copy(
            gram_h.at[pl.ds(pl.multiple_of(i * mb, mb), mb), pl.ds(pl.multiple_of(g * kw, kw), kw)],
            gram.at[n], gram_sem.at[n])

    store_copy = pltpu.make_async_copy(store_h, store, store_sem.at[0])

    barrier = pltpu.get_barrier_semaphore()
    for d in range(1, rows):
        pl.semaphore_signal(barrier, inc=1, device_id=dev(g, lax.rem(r + d, rows), c, s),
                            device_id_type=pl.DeviceIdType.MESH)
    for d in range(1, slices):
        pl.semaphore_signal(barrier, inc=1, device_id=dev(*at_spot(lax.rem(spot + d, slices))),
                            device_id_type=pl.DeviceIdType.MESH)

    def rs_copy(side, q, w):
        return remote(send.at[q, w], recv.at[side, q, w], rs_send.at[q, w], rs_recv.at[side, q, w],
                      g, lower if side else upper, c, s)

    def pass_on(side, q, w, value):
        send[q, w] = encode(value, 4, ps)
        rs_copy(side, q, w).start()

    for l in loads:
        l.wait()
    pl.semaphore_wait(barrier, rows - 1 + slices - 1)

    def project(i, _):
        q = pick(i)
        for w, (l, x, y) in enumerate(zip(load(i), (acts, grads), (pin, pout))):
            l.wait()
            value = jnp.dot(x[q], y[...], preferred_element_type=F32)
            part[q, w] = value

            @pl.when(jnp.logical_and(r == 0, q >= hi))
            def _():
                pass_on(0, q, w, value)

            @pl.when(jnp.logical_and(r == rows - 1, q < lo))
            def _():
                pass_on(1, q, w, value)
        return 0

    lax.fori_loop(0, queries, project, 0)
    for n in range(blocks):
        gram_copy(n).start()
    store_copy.start()

    def fx_copy(i, d):
        o = lax.rem(spot + d, slices)
        return remote(fsend.at[i, o], fbuf.at[lo + i, source], fx_send.at[i, d], fx_recv.at[i, d], *at_spot(o))

    def fx_own(i):
        return pltpu.make_async_copy(fsend.at[i, spot], fbuf.at[lo + i, source], fx_local.at[i])

    def fz_copy(side, q):
        return remote(fbuf.at[q], fbuf.at[q], fz_send.at[side, q], fz_recv.at[q],
                      g, lower if side else upper, c, s)

    def sums(t, _):
        for side in range(2):
            j = t - LAG * (rows - 1 - r if side else r)
            w = lax.rem(j, 2)
            q = j // 2 if side else queries - 1 - j // 2
            if side:
                live = jnp.logical_and(r < rows - 1, jnp.logical_and(j >= 0, q < hi))
                onward = q < lo
            else:
                live = jnp.logical_and(r > 0, jnp.logical_and(j >= 0, q >= lo))
                onward = q >= hi

            @pl.when(live)
            def _():
                rs_copy(side, q, w).wait_recv()
                value = part[q, w] + decode(recv[side, q, w], 4, ps)

                @pl.when(onward)
                def _():
                    pass_on(side, q, w, value)

                @pl.when(jnp.logical_not(onward))
                def _():
                    part[q, w] = value

        for i in range(homes):
            q = lo + i
            up = jnp.where(r > 0, LAG * r + 2 * (queries - 1 - q) + 1, 0)
            down = jnp.where(r < rows - 1, LAG * (rows - 1 - r) + 2 * q + 1, 0)

            @pl.when(jnp.logical_and(q < hi, t == jnp.maximum(up, down)))
            def _():
                ah, al = split(part[q, 0].T)
                gh, gl = split(part[q, 1])
                f = jnp.dot(jnp.concatenate([ah, al, ah], axis=1), jnp.concatenate([gh, gh, gl], axis=0),
                            preferred_element_type=F32)
                fsend[i] = encode(f.reshape(slices, aw, kout), 3, fs)
                for d in range(1, slices):
                    fx_copy(i, d).start()
                fx_own(i).start()
        return 0

    span = max(LAG * k + 2 * (queries - -(-k * queries // rows)) for k in range(rows))
    lax.fori_loop(LAG, span, sums, 0)

    def unpack(q):
        feats[:, q] = decode(fbuf[q], 3, fs)

    for i in range(homes):
        @pl.when(lo + i < hi)
        def _():
            for d in range(1, slices):
                fx_copy(i, d).wait_recv()
            fx_own(i).wait()

            @pl.when(r < rows - 1)
            def _():
                fz_copy(0, lo + i).start()

            @pl.when(r > 0)
            def _():
                fz_copy(1, lo + i).start()
            unpack(lo + i)

    def gather(d, _):
        for i in range(homes):
            for side in range(2):
                h = r + d if side else r - d
                q = first(h) + i

                @pl.when(jnp.logical_and(jnp.logical_and(h >= 0, h < rows), q < first(h + 1)))
                def _():
                    fz_copy(side, q).wait_recv()

                    @pl.when((r > 0) if side else (r < rows - 1))
                    def _():
                        fz_copy(side, q).start()
                    unpack(q)
        return 0

    lax.fori_loop(1, rows, gather, 0)

    width = ft.shape[1]
    allq = groups * nq
    for a in range(aw):
        x = feats[:, :, a, :].reshape(allq, kout)
        xh, xl = split(x)
        rest = [jnp.zeros((width - 2 * allq, kout), F32)] if width > 2 * allq else []
        y = jnp.concatenate([xh.astype(F32), xl.astype(F32)] + rest, axis=0)
        ft[a * kout:(a + 1) * kout, :] = y.T.astype(BF16)

    def sub_copy(p):
        return remote(pre.at[p], sub_in.at[p], ps_send.at[p], ps_recv.at[p], g, r, c, other)

    def y_copy(p, d):
        o = lax.rem(g + d, groups)
        return remote(ysend.at[p, o], yin.at[p, d], py_send.at[p, d], py_recv.at[p, d], o, r, c, s)

    def x_copy(p, d):
        return remote(xsend.at[p], xin.at[p, d], pc_send.at[p, d], pc_recv.at[p, d], g, r, lax.rem(c + d, cols), s)

    def product(n):
        gram_copy(n).wait()
        acc = jnp.dot(gram[n].astype(BF16), ft[...], preferred_element_type=F32)
        t = acc.T
        return t[:allq] + t[allq:2 * allq]

    for n in range(per):
        pre[n] = product(n)
        for k in range(subs - 1):
            sub_copy(n).start()

    def give(p):
        value = product(per + p)
        sub_copy(p).wait_recv()
        value = (value + sub_in[p]).reshape(groups, nq, mb)
        tot[p] = value
        ysend[p] = encode(value, 2, gs)
        for d in range(1, groups):
            y_copy(p, d).start()

    def across(p):
        value = tot[p, g]
        for d in range(1, groups):
            y_copy(p, d).wait_recv()
            value = value + decode(yin[p, d], 2, gs)
        tot[p, g] = value
        xsend[p] = encode(value, 2, gs)
        for d in range(1, cols):
            x_copy(p, d).start()

    def score_of(p):
        value = tot[p, g]
        for d in range(1, cols):
            x_copy(p, d).wait_recv()
            value = value + decode(xin[p, d], 2, gs)
        return lax.dot_general(jnp.concatenate(split(value), axis=0), store[:, p * mb:(p + 1) * mb],
                               (((1,), (1,)), ((), ())), preferred_element_type=F32)

    for p in range(per):
        give(p)
    store_copy.wait()
    for p in range(per):
        across(p)
    score = None
    for p in range(per):
        term = score_of(p)
        score = term if score is None else score + term
    score = score[:nq] + score[nq:]

    hq = nq // subs
    for o in range(subs):
        own[o] = score[o * hq:(o + 1) * hq]
    x_half = remote(own.at[other], half_in, ss_sem.at[0], ss_sem.at[1], g, r, c, other)
    x_half.start()
    x_half.wait()
    own_s[...] = own[s] + half_in[...]
    x_rows = [remote(own_s, half_all.at[r], sz_send.at[d], sz_recv.at[d], g, lax.rem(r + d, rows), c, s)
              for d in range(1, rows)]
    for x in x_rows:
        x.start()
    half_all[r] = own_s[...]
    for x in x_rows:
        x.wait()
    total = half_all[0]
    for o in range(1, rows):
        total = total + half_all[o]
    half_out[s] = total
    x_out = remote(half_out.at[s], half_out.at[s], sf_sem.at[0], sf_sem.at[1], g, r, c, other)
    x_out.start()

    for p in range(per):
        sub_copy(p).wait_send()
        for d in range(1, groups):
            y_copy(p, d).wait_send()
        for d in range(1, cols):
            x_copy(p, d).wait_send()
    for i in range(homes):
        @pl.when(lo + i < hi)
        def _():
            for d in range(1, slices):
                fx_copy(i, d).wait_send()

    def drain(q, _):
        @pl.when(jnp.logical_and(r < rows - 1, q < hi))
        def _():
            fz_copy(0, q).wait_send()

        @pl.when(jnp.logical_and(r > 0, q >= lo))
        def _():
            fz_copy(1, q).wait_send()

        for side, gone in enumerate((q >= hi, q < lo)):
            @pl.when(gone)
            def _():
                for w in range(2):
                    rs_copy(side, q, w).wait_send()
        return 0

    lax.fori_loop(0, queries, drain, 0)
    x_out.wait()
    for o in range(subs):
        out[o * hq:(o + 1) * hq, :] = half_out[o]


def body(sizes, query_acts, query_grads, proj_in, proj_out, inverse_gram, store_slab):
    groups, rows, cols, subs = sizes
    queries, tokens, depth = query_acts.shape
    kin, kout = proj_in.shape[1], proj_out.shape[1]
    planes = cols * subs
    slices = groups * planes
    nq = planes * queries
    aw = kin // slices
    grows, gcols = inverse_gram.shape
    kw = gcols // groups
    mb = min(512, grows // subs)
    blocks = grows // mb
    per = blocks // subs
    examples = store_slab.shape[0]
    hq = nq // subs
    homes = -(-queries // rows)
    dma = pltpu.SemaphoreType.DMA
    lanes = -(-2 * groups * nq // 128) * 128
    scratch = [
        pltpu.VMEM(query_acts.shape, BF16), pltpu.VMEM(query_grads.shape, BF16),
        pltpu.VMEM(proj_in.shape, BF16), pltpu.VMEM(proj_out.shape, BF16),
        pltpu.VMEM((blocks, mb, kw), F32), pltpu.VMEM(store_slab.shape, BF16),
        pltpu.VMEM((queries, 2, tokens, kin), F32), pltpu.VMEM((queries, 2, tokens, kin), BF16),
        pltpu.VMEM((2, queries, 2, tokens, kin), BF16),
        pltpu.VMEM((homes, slices, aw, kout), BF16), pltpu.VMEM((queries, slices, aw, kout), BF16),
        pltpu.VMEM((slices, queries, aw, kout), F32), pltpu.VMEM((kw, lanes), BF16),
        pltpu.VMEM((per, groups * nq, mb), F32), pltpu.VMEM((per, groups * nq, mb), F32),
        pltpu.VMEM((per, groups, nq, mb), F32),
        pltpu.VMEM((per, groups, nq, mb), BF16), pltpu.VMEM((per, groups, nq, mb), BF16),
        pltpu.VMEM((per, nq, mb), BF16), pltpu.VMEM((per, cols, nq, mb), BF16),
        pltpu.VMEM((subs, hq, examples), F32), pltpu.VMEM((hq, examples), F32), pltpu.VMEM((hq, examples), F32),
        pltpu.VMEM((rows, hq, examples), F32), pltpu.VMEM((subs, hq, examples), F32),
        dma((2,)), dma((queries, 2)), dma((blocks,)), dma((1,)), dma((queries, 2)), dma((2, queries, 2)),
        dma((homes, slices)), dma((homes, slices)), dma((homes,)), dma((2, queries)), dma((queries,)),
        dma((per,)), dma((per,)), dma((per, groups)), dma((per, groups)), dma((per, cols)), dma((per, cols)),
        dma((2,)), dma((rows,)), dma((rows,)), dma((2,)),
    ]
    return pl.pallas_call(
        functools.partial(kernel, groups, rows, cols, subs),
        out_shape=jax.ShapeDtypeStruct((nq, examples), F32),
        in_specs=[pl.BlockSpec(memory_space=pltpu.HBM)] * 6,
        out_specs=pl.BlockSpec(memory_space=pltpu.VMEM),
        scratch_shapes=scratch,
        compiler_params=pltpu.CompilerParams(
            collective_id=0, has_side_effects=True, vmem_limit_bytes=67043328),
        name="influence",
    )(query_acts, query_grads, proj_in, proj_out, inverse_gram, store_slab)


def solution(mesh):
    sizes = tuple(mesh.shape[n] for n in ("groups", "row", "col", "sub"))
    return jax.shard_map(
        functools.partial(body, sizes),
        mesh=mesh,
        in_specs=(
            P(("groups", "col", "sub"), None, "row"),
            P(("groups", "col", "sub"), None, "row"),
            P("row", None),
            P("row", None),
            P("row", ("col", "sub")),
            P(("groups", "col"), ("row", "sub")),
        ),
        out_specs=P("groups", "col"),
        check_vma=False,
    )
```

```python
import functools
import math

import jax
import jax.numpy as jnp
from jax import lax
from jax.experimental import pallas as pl
from jax.experimental.pallas import tpu as pltpu
from jax.sharding import PartitionSpec as P

F32, BF16 = jnp.float32, jnp.bfloat16
ACT_MAX, GRAD_MAX, PROJ_MAX, GRAM_MAX = 6.0, 0.5390625, 0.09375, 2.01


def split(x):
    hi = x.astype(BF16)
    return hi, (x - hi.astype(F32)).astype(BF16)


def scale_of(p, bound):
    return 2.0 ** math.floor(126 / p - math.log2(bound))


def encode(x, p, scale):
    z = x * scale
    if p == 2:
        y = z * jnp.abs(z)
    elif p == 3:
        y = z * z * z
    else:
        y = (z * z) * (z * jnp.abs(z))
    return y.astype(BF16)


def decode(y, p, scale):
    y = y.astype(F32)
    m = jnp.abs(y)
    if p == 2:
        v = m * lax.rsqrt(m) * (1.0 / scale)
    elif p == 3:
        v = jnp.exp2(jnp.log2(m) * (1.0 / 3.0)) * (1.0 / scale)
    else:
        v = lax.rsqrt(lax.rsqrt(m)) * (1.0 / scale)
    return jnp.where(y > 0, v, jnp.where(y < 0, -v, 0.0))


def each(n, fn):
    if n <= 8:
        for i in range(n):
            fn(i)
    else:
        def step(i, _):
            fn(i)
            return 0
        lax.fori_loop(0, n, step, 0)


def kernel(groups, rows, cols, subs, acts_h, grads_h, pin_h, pout_h, gram_h, store_h, out,
           acts, grads, pin, pout, gram, store, part, send, relay, recv, fsend, fbuf, feats, ft,
           pre, sub_in, tot, vsend, vin, own, own_s, half_in, half_all, half_out,
           p_sem, in_sem, gram_sem, store_sem, rs_send, rl_recv, rh_recv, fx_send, fx_recv,
           ps_send, ps_recv, pv_send, pv_recv, ss_sem, sz_send, sz_recv, sf_sem):
    g, r, c, s = (lax.axis_index(n) for n in ("groups", "row", "col", "sub"))
    queries, tokens, depth = acts.shape
    planes = cols * subs
    slices = groups * planes
    me = c * subs + s
    spot = me * groups + g
    source = g * planes + me
    aw, kout = feats.shape[2], feats.shape[3]
    kin = pin.shape[1]
    blocks, mb, kw = gram.shape
    per = blocks // subs
    other = lax.rem(s + 1, subs)
    nq = planes * queries
    homes = fsend.shape[0]
    act_bound = rows * depth * ACT_MAX * PROJ_MAX
    grad_bound = rows * depth * GRAD_MAX * PROJ_MAX
    feat_bound = tokens * act_bound * grad_bound
    ps = scale_of(4, max(act_bound, grad_bound))
    fs = scale_of(3, feat_bound)
    gs = scale_of(2, feat_bound * GRAM_MAX * gram_h.shape[1] * planes)

    def dev(group, row, col, sub):
        return {"groups": group, "row": row, "col": col, "sub": sub}

    def remote(src, dst, snd, rcv, group, row, col, sub):
        return pltpu.make_async_remote_copy(
            src_ref=src, dst_ref=dst, send_sem=snd, recv_sem=rcv,
            device_id=dev(group, row, col, sub), device_id_type=pl.DeviceIdType.MESH)

    def at_spot(o, row):
        plane = o // groups
        return lax.rem(o, groups), row, plane // subs, lax.rem(plane, subs)

    def first(row):
        return (row * queries + rows - 1) // rows

    def when_some(h, fn):
        def run():
            fn()

        if queries % rows == 0:
            run()
        else:
            pl.when(first(h) < first(h + 1))(run)

    odd = lax.rem(r, 2)
    pair = r // 2
    partner = r + 1 - 2 * odd

    def target(i):
        h = jnp.where(odd == 1, jnp.where(i < r, i, rows - 1 - i + r),
                      jnp.where(i < rows - 1 - r, rows - 1 - i, i - (rows - 1 - r)))
        return jnp.where(i == rows - 1, r, h)

    def relays(h):
        return jnp.where(odd == 1, h > r, h < r)

    loads = [pltpu.make_async_copy(pin_h, pin, p_sem.at[0]), pltpu.make_async_copy(pout_h, pout, p_sem.at[1])]

    def load(h, w):
        q = pl.ds(first(h), homes)
        return pltpu.make_async_copy((acts_h, grads_h)[w].at[q], (acts, grads)[w].at[q], in_sem.at[h, w])

    for w in range(2):
        loads[w].start()
        when_some(target(0), lambda: load(target(0), w).start())

    def more(i):
        h = target(i + 1)
        when_some(h, lambda: [load(h, w).start() for w in range(2)])

    each(rows - 1, more)

    def gram_copy(n):
        i = (other if n % subs == 0 else s) * per + n // subs
        return pltpu.make_async_copy(
            gram_h.at[pl.ds(pl.multiple_of(i * mb, mb), mb), pl.ds(pl.multiple_of(g * kw, kw), kw)],
            gram.at[n], gram_sem.at[n])

    store_copy = pltpu.make_async_copy(store_h, store, store_sem.at[0])

    barrier = pltpu.get_barrier_semaphore()
    everyone = rows * slices

    def greet(d):
        o = lax.rem(r * slices + spot + d + 1, everyone)
        group, row, col, sub = at_spot(lax.rem(o, slices), o // slices)
        pl.semaphore_signal(barrier, inc=1, device_id=dev(group, row, col, sub), device_id_type=pl.DeviceIdType.MESH)

    lax.fori_loop(0, everyone - 1, lambda d, z: (greet(d), z)[1], 0)

    def relay_copy(w, q):
        return remote(send.at[w, q], relay.at[w, q], rs_send.at[w, q], rl_recv.at[w, q], g, partner, c, s)

    def home_copy(w, h, k):
        q = first(h) + k
        return remote(send.at[w, q], recv.at[pair, w, k], rs_send.at[w, q], rh_recv.at[pair, w, k], g, h, c, s)

    def project(i):
        h = target(i)

        def _():
            q = pl.ds(first(h), homes)
            for w, (x, y) in enumerate(((acts, pin), (grads, pout))):
                if isinstance(i, int) and i == 0:
                    loads[w].wait()
                load(h, w).wait()
                value = jnp.dot(x[q].reshape(homes * tokens, depth), y[...],
                                preferred_element_type=F32).reshape(homes, tokens, kin)
                part[w, q] = value
                if isinstance(i, int) and i == 0 and w == 0:
                    pl.semaphore_wait(barrier, everyone - 1)

                @pl.when(jnp.logical_not(jnp.logical_or(h == r, relays(h))))
                def _():
                    send[w, q] = encode(value, 4, ps)
                    for k in range(homes):
                        @pl.when(h == partner)
                        def _():
                            home_copy(w, h, k).start()

                        @pl.when(h != partner)
                        def _():
                            relay_copy(w, first(h) + k).start()

        when_some(h, _)

    if rows > 8:
        for l in loads:
            l.wait()
        pl.semaphore_wait(barrier, everyone - 1)
    each(rows, project)
    for n in range(blocks):
        gram_copy(n).start()
    store_copy.start()

    def forward(i):
        h = target(i)

        def _():
            @pl.when(relays(h))
            def _():
                for w in range(2):
                    for k in range(homes):
                        q = first(h) + k
                        relay_copy(w, q).wait_recv()
                        send[w, q] = encode(part[w, q] + decode(relay[w, q], 4, ps), 4, ps)
                        home_copy(w, h, k).start()

        @pl.when(h != partner)
        def _():
            when_some(h, _)

    each(rows - 1, forward)

    def fx_copy(k, row, o):
        return remote(fsend.at[k, o], fbuf.at[first(r) + k, source], fx_send.at[k, row, o],
                      fx_recv.at[first(r) + k], *at_spot(o, row))

    def fx_own(k):
        return pltpu.make_async_copy(fsend.at[k, spot], fbuf.at[first(r) + k, source], fx_recv.at[first(r) + k])

    def users(k, use):
        def row_of(j):
            row = jnp.where(2 * r < rows, rows - 1 - j, j)

            def slice_of(d):
                o = lax.rem(spot + d, slices)

                @pl.when(jnp.logical_or(row != r, o != spot))
                def _():
                    use(fx_copy(k, row, o))

            each(slices, slice_of)

        each(rows, row_of)

    def final():
        for k in range(homes):
            q = first(r) + k
            sides = []
            for w in range(2):
                value = part[w, q]
                for o in range(rows // 2):
                    remote(send.at[w, q], recv.at[o, w, k], rs_send.at[w, q], rh_recv.at[o, w, k],
                           g, partner, c, s).wait_recv()
                    value = value + decode(recv[o, w, k], 4, ps)
                sides.append(value)
            ah, al = split(sides[0].T)
            gh, gl = split(sides[1])
            f = jnp.dot(jnp.concatenate([ah, al, ah], axis=1), jnp.concatenate([gh, gh, gl], axis=0),
                        preferred_element_type=F32)
            fsend[k] = encode(f.reshape(slices, aw, kout), 3, fs)
            users(k, lambda copy: copy.start())
            fx_own(k).start()

    when_some(r, final)

    for q in range(queries):
        remote(fbuf.at[q], fbuf.at[q], fx_send.at[0, 0, 0], fx_recv.at[q], g, partner, c, s).wait_recv()
        feats[:, q] = decode(fbuf[q], 3, fs)

    width = ft.shape[1]
    allq = groups * nq
    for a in range(aw):
        x = feats[:, :, a, :].reshape(allq, kout)
        xh, xl = split(x)
        rest = [jnp.zeros((width - 2 * allq, kout), F32)] if width > 2 * allq else []
        y = jnp.concatenate([xh.astype(F32), xl.astype(F32)] + rest, axis=0)
        ft[a * kout:(a + 1) * kout, :] = y.T.astype(BF16)

    def sub_copy(p):
        return remote(pre.at[p], sub_in.at[p], ps_send.at[p], ps_recv.at[p], g, r, c, other)

    spread = groups * cols
    mine = g * cols + c

    def v_copy(p, d):
        o = lax.rem(mine + d, spread)
        return remote(vsend.at[p, o // cols], vin.at[p, d], pv_send.at[p, d], pv_recv.at[p, d],
                      o // cols, r, lax.rem(o, cols), s)

    def product(n):
        gram_copy(n).wait()
        acc = jnp.dot(gram[n].astype(BF16), ft[...], preferred_element_type=F32)
        t = acc.T
        return t[:allq] + t[allq:2 * allq]

    for p in range(per):
        pre[p] = product(subs * p)
        sub_copy(p).start()
        value = product(subs * p + 1)
        sub_copy(p).wait_recv()
        value = (value + sub_in[p]).reshape(groups, nq, mb)
        tot[p] = value
        vsend[p] = encode(value, 2, gs)
        for d in range(1, spread):
            v_copy(p, d).start()
    store_copy.wait()
    score = None
    for p in range(per):
        value = tot[p, g]
        for d in range(1, spread):
            v_copy(p, d).wait_recv()
            value = value + decode(vin[p, d], 2, gs)
        term = lax.dot_general(jnp.concatenate(split(value), axis=0), store[:, p * mb:(p + 1) * mb],
                               (((1,), (1,)), ((), ())), preferred_element_type=F32)
        score = term if score is None else score + term
    score = score[:nq] + score[nq:]

    hq = nq // subs
    for o in range(subs):
        own[o] = score[o * hq:(o + 1) * hq]
    x_half = remote(own.at[other], half_in, ss_sem.at[0], ss_sem.at[1], g, r, c, other)
    x_half.start()
    x_half.wait()
    own_s[...] = own[s] + half_in[...]
    x_rows = [remote(own_s, half_all.at[r], sz_send.at[d], sz_recv.at[d], g, lax.rem(r + d, rows), c, s)
              for d in range(1, rows)]
    for x in x_rows:
        x.start()
    half_all[r] = own_s[...]
    for p in range(per):
        sub_copy(p).wait_send()
        for d in range(1, spread):
            v_copy(p, d).wait_send()
    when_some(r, lambda: [users(k, lambda copy: copy.wait_send()) for k in range(homes)])

    def drain(i):
        h = target(i)

        def _():
            for w in range(2):
                for k in range(homes):
                    relay_copy(w, first(h) + k).wait_send()

        when_some(h, _)

    each(rows - 1, drain)
    for x in x_rows:
        x.wait()
    total = half_all[0]
    for o in range(1, rows):
        total = total + half_all[o]
    half_out[s] = total
    x_out = remote(half_out.at[s], half_out.at[s], sf_sem.at[0], sf_sem.at[1], g, r, c, other)
    x_out.start()
    x_out.wait()
    for o in range(subs):
        out[o * hq:(o + 1) * hq, :] = half_out[o]


def body(sizes, query_acts, query_grads, proj_in, proj_out, inverse_gram, store_slab):
    groups, rows, cols, subs = sizes
    queries, tokens, depth = query_acts.shape
    kin, kout = proj_in.shape[1], proj_out.shape[1]
    planes = cols * subs
    slices = groups * planes
    nq = planes * queries
    aw = kin // slices
    grows, gcols = inverse_gram.shape
    kw = gcols // groups
    mb = min(512, grows // subs)
    blocks = grows // mb
    per = blocks // subs
    spread = groups * cols
    examples = store_slab.shape[0]
    hq = nq // subs
    homes = -(-queries // rows)
    assert rows % 2 == 0 and subs == 2 and (queries % rows == 0 or rows % queries == 0)
    dma = pltpu.SemaphoreType.DMA
    lanes = -(-2 * groups * nq // 128) * 128
    scratch = [
        pltpu.VMEM(query_acts.shape, BF16), pltpu.VMEM(query_grads.shape, BF16),
        pltpu.VMEM(proj_in.shape, BF16), pltpu.VMEM(proj_out.shape, BF16),
        pltpu.VMEM((blocks, mb, kw), F32), pltpu.VMEM(store_slab.shape, BF16),
        pltpu.VMEM((2, queries, tokens, kin), F32), pltpu.VMEM((2, queries, tokens, kin), BF16),
        pltpu.VMEM((2, queries, tokens, kin), BF16), pltpu.VMEM((rows // 2, 2, homes, tokens, kin), BF16),
        pltpu.VMEM((homes, slices, aw, kout), BF16), pltpu.VMEM((queries, slices, aw, kout), BF16),
        pltpu.VMEM((slices, queries, aw, kout), F32), pltpu.VMEM((kw, lanes), BF16),
        pltpu.VMEM((per, groups * nq, mb), F32), pltpu.VMEM((per, groups * nq, mb), F32),
        pltpu.VMEM((per, groups, nq, mb), F32),
        pltpu.VMEM((per, groups, nq, mb), BF16), pltpu.VMEM((per, spread, nq, mb), BF16),
        pltpu.VMEM((subs, hq, examples), F32), pltpu.VMEM((hq, examples), F32), pltpu.VMEM((hq, examples), F32),
        pltpu.VMEM((rows, hq, examples), F32), pltpu.VMEM((subs, hq, examples), F32),
        dma((2,)), dma((rows, 2)), dma((blocks,)), dma((1,)), dma((2, queries)), dma((2, queries)),
        dma((rows // 2, 2, homes)), dma((homes, rows, slices)), dma((queries,)),
        dma((per,)), dma((per,)), dma((per, spread)), dma((per, spread)),
        dma((2,)), dma((rows,)), dma((rows,)), dma((2,)),
    ]
    return pl.pallas_call(
        functools.partial(kernel, groups, rows, cols, subs),
        out_shape=jax.ShapeDtypeStruct((nq, examples), F32),
        in_specs=[pl.BlockSpec(memory_space=pltpu.HBM)] * 6,
        out_specs=pl.BlockSpec(memory_space=pltpu.VMEM),
        scratch_shapes=scratch,
        compiler_params=pltpu.CompilerParams(
            collective_id=0, has_side_effects=True, vmem_limit_bytes=67043328),
        name="influence",
    )(query_acts, query_grads, proj_in, proj_out, inverse_gram, store_slab)


def solution(mesh):
    sizes = tuple(mesh.shape[n] for n in ("groups", "row", "col", "sub"))
    return jax.shard_map(
        functools.partial(body, sizes),
        mesh=mesh,
        in_specs=(
            P(("groups", "col", "sub"), None, "row"),
            P(("groups", "col", "sub"), None, "row"),
            P("row", None),
            P("row", None),
            P("row", ("col", "sub")),
            P(("groups", "col"), ("row", "sub")),
        ),
        out_specs=P("groups", "col"),
        check_vma=False,
    )
```

```python
import functools
import math

import jax
import jax.numpy as jnp
from jax import lax
from jax.experimental import pallas as pl
from jax.experimental.pallas import tpu as pltpu
from jax.sharding import PartitionSpec as P

F32, BF16 = jnp.float32, jnp.bfloat16
ACT_MAX, GRAD_MAX, PROJ_MAX, GRAM_MAX, STORE_MAX = 6.0, 0.5390625, 0.09375, 2.01, 0.046875


def split(x):
    hi = x.astype(BF16)
    return hi, (x - hi.astype(F32)).astype(BF16)


def scale_of(p, bound):
    return 2.0 ** math.floor(126 / p - math.log2(bound))


def encode(x, p, scale):
    z = x * scale
    if p == 2:
        y = z * jnp.abs(z)
    elif p == 3:
        y = z * z * z
    else:
        y = (z * z) * (z * jnp.abs(z))
    return y.astype(BF16)


def decode(y, p, scale):
    y = y.astype(F32)
    m = jnp.abs(y)
    if p == 2:
        v = m * lax.rsqrt(m) * (1.0 / scale)
    elif p == 3:
        v = jnp.exp2(jnp.log2(m) * (1.0 / 3.0)) * (1.0 / scale)
    else:
        v = lax.rsqrt(lax.rsqrt(m)) * (1.0 / scale)
    return jnp.where(y > 0, v, jnp.where(y < 0, -v, 0.0))


def each(n, fn):
    if n <= 8:
        for i in range(n):
            fn(i)
    else:
        def step(i, _):
            fn(i)
            return 0
        lax.fori_loop(0, n, step, 0)


def kernel(groups, rows, cols, subs, acts_h, grads_h, pin_h, pout_h, gram_h, store_h, out,
           acts, grads, pin, pout, gram, store, part, send, relay, recv, fsend, fbuf, feats, ft,
           pre, sub_in, tot, vsend, vin, own, own_s, half_in, half_all, half_out,
           p_sem, in_sem, gram_sem, store_sem, rs_send, rl_recv, rh_recv, fx_send, fx_recv,
           ps_send, ps_recv, pv_send, pv_recv, ss_sem, sz_send, sz_recv, sf_sem):
    g, r, c, s = (lax.axis_index(n) for n in ("groups", "row", "col", "sub"))
    queries, tokens, depth = acts.shape
    planes = cols * subs
    slices = groups * planes
    me = c * subs + s
    spot = me * groups + g
    source = g * planes + me
    aw, kout = feats.shape[2], feats.shape[3]
    kin = pin.shape[1]
    blocks, mb, kw = gram.shape
    per = blocks // subs
    other = lax.rem(s + 1, subs)
    nq = planes * queries
    homes = fsend.shape[0]
    act_bound = rows * depth * ACT_MAX * PROJ_MAX
    grad_bound = rows * depth * GRAD_MAX * PROJ_MAX
    feat_bound = tokens * act_bound * grad_bound
    ps = scale_of(4, max(act_bound, grad_bound))
    fs = scale_of(3, feat_bound)
    pre_bound = feat_bound * GRAM_MAX * gram_h.shape[1] * planes
    gs = scale_of(2, pre_bound)
    zs = scale_of(2, pre_bound * STORE_MAX * gram_h.shape[1] * planes)

    def dev(group, row, col, sub):
        return {"groups": group, "row": row, "col": col, "sub": sub}

    def remote(src, dst, snd, rcv, group, row, col, sub):
        return pltpu.make_async_remote_copy(
            src_ref=src, dst_ref=dst, send_sem=snd, recv_sem=rcv,
            device_id=dev(group, row, col, sub), device_id_type=pl.DeviceIdType.MESH)

    def at_spot(o, row):
        plane = o // groups
        return lax.rem(o, groups), row, plane // subs, lax.rem(plane, subs)

    def first(row):
        return (row * queries + rows - 1) // rows

    def when_some(h, fn):
        def run():
            fn()

        if queries % rows == 0:
            run()
        else:
            pl.when(first(h) < first(h + 1))(run)

    odd = lax.rem(r, 2)
    pair = r // 2
    partner = r + 1 - 2 * odd

    def target(i):
        h = jnp.where(odd == 1, jnp.where(i < r, i, rows - 1 - i + r),
                      jnp.where(i < rows - 1 - r, rows - 1 - i, i - (rows - 1 - r)))
        return jnp.where(i == rows - 1, r, h)

    def relays(h):
        return jnp.where(odd == 1, h > r, h < r)

    loads = [pltpu.make_async_copy(pin_h, pin, p_sem.at[0]), pltpu.make_async_copy(pout_h, pout, p_sem.at[1])]

    def load(h, w):
        q = pl.ds(first(h), homes)
        return pltpu.make_async_copy((acts_h, grads_h)[w].at[q], (acts, grads)[w].at[q], in_sem.at[h, w])

    for w in range(2):
        loads[w].start()
        when_some(target(0), lambda: load(target(0), w).start())

    barrier = pltpu.get_barrier_semaphore()

    def greet(*place):
        pl.semaphore_signal(barrier, inc=1, device_id=dev(*place), device_id_type=pl.DeviceIdType.MESH)

    for d in range(1, slices):
        greet(*at_spot(lax.rem(spot + d, slices), r))
    for d in range(1, rows):
        greet(g, lax.rem(r + d, rows), c, s)
    guests = slices - 1 + rows - 1

    def more(i):
        h = target(i + 1)
        when_some(h, lambda: [load(h, w).start() for w in range(2)])

    each(rows - 1, more)

    def gram_copy(n):
        i = (other if n % subs == 0 else s) * per + n // subs
        return pltpu.make_async_copy(
            gram_h.at[pl.ds(pl.multiple_of(i * mb, mb), mb), pl.ds(pl.multiple_of(g * kw, kw), kw)],
            gram.at[n], gram_sem.at[n])

    store_copy = pltpu.make_async_copy(store_h, store, store_sem.at[0])

    def relay_copy(w, q):
        return remote(send.at[w, q], relay.at[w, q], rs_send.at[w, q], rl_recv.at[w, q], g, partner, c, s)

    def home_copy(w, h, k):
        q = first(h) + k
        return remote(send.at[w, q], recv.at[pair, w, k], rs_send.at[w, q], rh_recv.at[pair, w, k], g, h, c, s)

    def project(i):
        h = target(i)

        def _():
            q = pl.ds(first(h), homes)
            for w, (x, y) in enumerate(((acts, pin), (grads, pout))):
                if isinstance(i, int) and i == 0:
                    loads[w].wait()
                load(h, w).wait()
                value = jnp.dot(x[q].reshape(homes * tokens, depth), y[...],
                                preferred_element_type=F32).reshape(homes, tokens, kin)
                part[w, q] = value
                if isinstance(i, int) and i == 0 and w == 0:
                    pl.semaphore_wait(barrier, guests)

                @pl.when(jnp.logical_not(jnp.logical_or(h == r, relays(h))))
                def _():
                    send[w, q] = encode(value, 4, ps)
                    for k in range(homes):
                        @pl.when(h == partner)
                        def _():
                            home_copy(w, h, k).start()

                        @pl.when(h != partner)
                        def _():
                            relay_copy(w, first(h) + k).start()

        when_some(h, _)

    if rows > 8:
        for l in loads:
            l.wait()
        pl.semaphore_wait(barrier, guests)
    each(rows, project)
    for n in range(blocks):
        gram_copy(n).start()
    store_copy.start()

    def forward(i):
        h = target(i)

        def _():
            @pl.when(relays(h))
            def _():
                for w in range(2):
                    for k in range(homes):
                        q = first(h) + k
                        relay_copy(w, q).wait_recv()
                        send[w, q] = encode(part[w, q] + decode(relay[w, q], 4, ps), 4, ps)
                        home_copy(w, h, k).start()

        @pl.when(h != partner)
        def _():
            when_some(h, _)

    each(rows - 1, forward)

    def fx_copy(k, row, o):
        return remote(fsend.at[k, o], fbuf.at[first(r) + k, source], fx_send.at[k, row, o],
                      fx_recv.at[first(r) + k], *at_spot(o, row))

    def fx_own(k):
        return pltpu.make_async_copy(fsend.at[k, spot], fbuf.at[first(r) + k, source], fx_recv.at[first(r) + k])

    def users(k, use):
        def slice_of(d):
            o = lax.rem(spot + d + 1, slices)

            def row_of(j):
                row = jnp.where(2 * r < rows, rows - 1 - j, j)
                if isinstance(d, int) and d < slices - 1:
                    use(fx_copy(k, row, o))
                else:
                    @pl.when(jnp.logical_or(row != r, o != spot))
                    def _():
                        use(fx_copy(k, row, o))

            each(rows, row_of)

        each(slices, slice_of)

    def final():
        for k in range(homes):
            q = first(r) + k
            sides = []
            for w in range(2):
                value = part[w, q]
                for o in range(rows // 2):
                    remote(send.at[w, q], recv.at[o, w, k], rs_send.at[w, q], rh_recv.at[o, w, k],
                           g, partner, c, s).wait_recv()
                    value = value + decode(recv[o, w, k], 4, ps)
                sides.append(value)
            ah, al = split(sides[0].T)
            gh, gl = split(sides[1])
            f = jnp.dot(jnp.concatenate([ah, al, ah], axis=1), jnp.concatenate([gh, gh, gl], axis=0),
                        preferred_element_type=F32)
            fsend[k] = encode(f.reshape(slices, aw, kout), 3, fs)
            users(k, lambda copy: copy.start())
            fx_own(k).start()

    when_some(r, final)

    for q in range(queries):
        remote(fbuf.at[q], fbuf.at[q], fx_send.at[0, 0, 0], fx_recv.at[q], g, partner, c, s).wait_recv()
        feats[:, q] = decode(fbuf[q], 3, fs)

    width = ft.shape[1]
    allq = groups * nq
    for a in range(aw):
        x = feats[:, :, a, :].reshape(allq, kout)
        xh, xl = split(x)
        rest = [jnp.zeros((width - 2 * allq, kout), F32)] if width > 2 * allq else []
        y = jnp.concatenate([xh.astype(F32), xl.astype(F32)] + rest, axis=0)
        ft[a * kout:(a + 1) * kout, :] = y.T.astype(BF16)

    def sub_copy(p):
        return remote(pre.at[p], sub_in.at[p], ps_send.at[p], ps_recv.at[p], g, r, c, other)

    spread = groups * cols
    mine = g * cols + c

    def v_copy(p, d):
        o = lax.rem(mine + d, spread)
        return remote(vsend.at[p, o // cols], vin.at[p, d], pv_send.at[p, d], pv_recv.at[p, d],
                      o // cols, r, lax.rem(o, cols), s)

    def product(n):
        gram_copy(n).wait()
        acc = jnp.dot(gram[n].astype(BF16), ft[...], preferred_element_type=F32)
        t = acc.T
        return t[:allq] + t[allq:2 * allq]

    def theirs(p):
        pre[p] = product(subs * p)
        sub_copy(p).start()

    def combine(p):
        sub_copy(p).wait_recv()
        value = (tot[p] + sub_in[p].reshape(groups, nq, mb))
        tot[p] = value
        vsend[p] = encode(value, 2, gs)
        for d in range(1, spread):
            v_copy(p, d).start()

    theirs(0)
    for p in range(per):
        if p + 1 < per:
            theirs(p + 1)
        tot[p] = product(subs * p + 1).reshape(groups, nq, mb)
        combine(p)
    store_copy.wait()
    score = None
    for p in range(per):
        value = tot[p, g]
        for d in range(1, spread):
            v_copy(p, d).wait_recv()
            value = value + decode(vin[p, d], 2, gs)
        term = lax.dot_general(jnp.concatenate(split(value), axis=0), store[:, p * mb:(p + 1) * mb],
                               (((1,), (1,)), ((), ())), preferred_element_type=F32)
        score = term if score is None else score + term
    score = score[:nq] + score[nq:]

    hq = nq // subs
    for o in range(subs):
        own[o] = score[o * hq:(o + 1) * hq]
    x_half = remote(own.at[other], half_in, ss_sem.at[0], ss_sem.at[1], g, r, c, other)
    x_half.start()
    x_half.wait()
    half = own[s] + half_in[...]
    own_s[...] = encode(half, 2, zs)
    x_rows = [remote(own_s, half_all.at[d], sz_send.at[d], sz_recv.at[d], g, lax.rem(r + d, rows), c, s)
              for d in range(1, rows)]
    for x in x_rows:
        x.start()
    half_in[...] = half
    for p in range(per):
        sub_copy(p).wait_send()
        for d in range(1, spread):
            v_copy(p, d).wait_send()
    when_some(r, lambda: [users(k, lambda copy: copy.wait_send()) for k in range(homes)])

    def drain(i):
        h = target(i)

        def _():
            for w in range(2):
                for k in range(homes):
                    relay_copy(w, first(h) + k).wait_send()

        when_some(h, _)

    each(rows - 1, drain)
    total = half_in[...]
    for d in range(1, rows):
        x_rows[d - 1].wait()
        total = total + decode(half_all[d], 2, zs)
    half_out[s] = total
    x_out = remote(half_out.at[s], half_out.at[s], sf_sem.at[0], sf_sem.at[1], g, r, c, other)
    x_out.start()
    x_out.wait()
    for o in range(subs):
        out[o * hq:(o + 1) * hq, :] = half_out[o]


def body(sizes, query_acts, query_grads, proj_in, proj_out, inverse_gram, store_slab):
    groups, rows, cols, subs = sizes
    queries, tokens, depth = query_acts.shape
    kin, kout = proj_in.shape[1], proj_out.shape[1]
    planes = cols * subs
    slices = groups * planes
    nq = planes * queries
    aw = kin // slices
    grows, gcols = inverse_gram.shape
    kw = gcols // groups
    mb = min(512, grows // subs)
    blocks = grows // mb
    per = blocks // subs
    spread = groups * cols
    examples = store_slab.shape[0]
    hq = nq // subs
    homes = -(-queries // rows)
    assert rows % 2 == 0 and subs == 2 and (queries % rows == 0 or rows % queries == 0)
    dma = pltpu.SemaphoreType.DMA
    lanes = -(-2 * groups * nq // 128) * 128
    scratch = [
        pltpu.VMEM(query_acts.shape, BF16), pltpu.VMEM(query_grads.shape, BF16),
        pltpu.VMEM(proj_in.shape, BF16), pltpu.VMEM(proj_out.shape, BF16),
        pltpu.VMEM((blocks, mb, kw), F32), pltpu.VMEM(store_slab.shape, BF16),
        pltpu.VMEM((2, queries, tokens, kin), F32), pltpu.VMEM((2, queries, tokens, kin), BF16),
        pltpu.VMEM((2, queries, tokens, kin), BF16), pltpu.VMEM((rows // 2, 2, homes, tokens, kin), BF16),
        pltpu.VMEM((homes, slices, aw, kout), BF16), pltpu.VMEM((queries, slices, aw, kout), BF16),
        pltpu.VMEM((slices, queries, aw, kout), F32), pltpu.VMEM((kw, lanes), BF16),
        pltpu.VMEM((per, groups * nq, mb), F32), pltpu.VMEM((per, groups * nq, mb), F32),
        pltpu.VMEM((per, groups, nq, mb), F32),
        pltpu.VMEM((per, groups, nq, mb), BF16), pltpu.VMEM((per, spread, nq, mb), BF16),
        pltpu.VMEM((subs, hq, examples), F32), pltpu.VMEM((hq, examples), BF16), pltpu.VMEM((hq, examples), F32),
        pltpu.VMEM((rows, hq, examples), BF16), pltpu.VMEM((subs, hq, examples), F32),
        dma((2,)), dma((rows, 2)), dma((blocks,)), dma((1,)), dma((2, queries)), dma((2, queries)),
        dma((rows // 2, 2, homes)), dma((homes, rows, slices)), dma((queries,)),
        dma((per,)), dma((per,)), dma((per, spread)), dma((per, spread)),
        dma((2,)), dma((rows,)), dma((rows,)), dma((2,)),
    ]
    return pl.pallas_call(
        functools.partial(kernel, groups, rows, cols, subs),
        out_shape=jax.ShapeDtypeStruct((nq, examples), F32),
        in_specs=[pl.BlockSpec(memory_space=pltpu.HBM)] * 6,
        out_specs=pl.BlockSpec(memory_space=pltpu.VMEM),
        scratch_shapes=scratch,
        compiler_params=pltpu.CompilerParams(
            collective_id=0, has_side_effects=True, vmem_limit_bytes=67043328),
        name="influence",
    )(query_acts, query_grads, proj_in, proj_out, inverse_gram, store_slab)


def solution(mesh):
    sizes = tuple(mesh.shape[n] for n in ("groups", "row", "col", "sub"))
    return jax.shard_map(
        functools.partial(body, sizes),
        mesh=mesh,
        in_specs=(
            P(("groups", "col", "sub"), None, "row"),
            P(("groups", "col", "sub"), None, "row"),
            P("row", None),
            P("row", None),
            P("row", ("col", "sub")),
            P(("groups", "col"), ("row", "sub")),
        ),
        out_specs=P("groups", "col"),
        check_vma=False,
    )
```

```python
import functools
import math

import jax
import jax.numpy as jnp
from jax import lax
from jax.experimental import pallas as pl
from jax.experimental.pallas import tpu as pltpu
from jax.sharding import PartitionSpec as P

F32, BF16 = jnp.float32, jnp.bfloat16
ACT_MAX, GRAD_MAX, PROJ_MAX, GRAM_MAX, STORE_MAX = 6.0, 0.5390625, 0.09375, 2.01, 0.046875


def split(x):
    hi = x.astype(BF16)
    return hi, (x - hi.astype(F32)).astype(BF16)


def scale_of(p, bound):
    return 2.0 ** math.floor(126 / p - math.log2(bound))


def encode(x, p, scale):
    z = x * scale
    if p == 2:
        y = z * jnp.abs(z)
    elif p == 3:
        y = z * z * z
    else:
        y = (z * z) * (z * jnp.abs(z))
    return y.astype(BF16)


def decode(y, p, scale):
    y = y.astype(F32)
    m = jnp.abs(y)
    if p == 2:
        v = m * lax.rsqrt(m) * (1.0 / scale)
    elif p == 3:
        v = jnp.exp2(jnp.log2(m) * (1.0 / 3.0)) * (1.0 / scale)
    else:
        v = lax.rsqrt(lax.rsqrt(m)) * (1.0 / scale)
    return jnp.where(y > 0, v, jnp.where(y < 0, -v, 0.0))


def each(n, fn):
    if n <= 8:
        for i in range(n):
            fn(i)
    else:
        def step(i, _):
            fn(i)
            return 0
        lax.fori_loop(0, n, step, 0)


def kernel(groups, rows, cols, subs, acts_h, grads_h, pin_h, pout_h, gram_h, store_h, out,
           acts, grads, pin, pout, gram, store, part, send, relay, recv, fsend, fbuf, feats, ft, early,
           pre, sub_in, tot, vsend, vin, own, own_s, half_in, half_all, half_out,
           p_sem, in_sem, gram_sem, store_sem, rs_send, rl_recv, rh_recv, fx_send, fx_recv,
           ps_send, ps_recv, pv_send, pv_recv, ss_sem, sz_send, sz_recv, sf_sem):
    g, r, c, s = (lax.axis_index(n) for n in ("groups", "row", "col", "sub"))
    queries, tokens, depth = acts.shape
    planes = cols * subs
    slices = groups * planes
    me = c * subs + s
    spot = me * groups + g
    source = g * planes + me
    aw, kout = feats.shape[2], feats.shape[3]
    kin = pin.shape[1]
    blocks, mb, kw = gram.shape
    per = blocks // subs
    other = lax.rem(s + 1, subs)
    nq = planes * queries
    parts, _, homes, az, _ = fsend.shape
    kz = kw // parts
    act_bound = rows * depth * ACT_MAX * PROJ_MAX
    grad_bound = rows * depth * GRAD_MAX * PROJ_MAX
    feat_bound = tokens * act_bound * grad_bound
    ps = scale_of(4, max(act_bound, grad_bound))
    fs = scale_of(3, feat_bound)
    pre_bound = feat_bound * GRAM_MAX * gram_h.shape[1] * planes
    gs = scale_of(2, pre_bound)
    zs = scale_of(2, pre_bound * STORE_MAX * gram_h.shape[1] * planes)

    def dev(group, row, col, sub):
        return {"groups": group, "row": row, "col": col, "sub": sub}

    def remote(src, dst, snd, rcv, group, row, col, sub):
        return pltpu.make_async_remote_copy(
            src_ref=src, dst_ref=dst, send_sem=snd, recv_sem=rcv,
            device_id=dev(group, row, col, sub), device_id_type=pl.DeviceIdType.MESH)

    def at_spot(o, row):
        plane = o // groups
        return lax.rem(o, groups), row, plane // subs, lax.rem(plane, subs)

    def first(row):
        return (row * queries + rows - 1) // rows

    def when_some(h, fn):
        def run():
            fn()

        if queries % rows == 0:
            run()
        else:
            pl.when(first(h) < first(h + 1))(run)

    odd = lax.rem(r, 2)
    pair = r // 2
    partner = r + 1 - 2 * odd

    def target(i):
        h = jnp.where(odd == 1, jnp.where(i < r, i, rows - 1 - i + r),
                      jnp.where(i < rows - 1 - r, rows - 1 - i, i - (rows - 1 - r)))
        return jnp.where(i == rows - 1, r, h)

    def relays(h):
        return jnp.where(odd == 1, h > r, h < r)

    loads = [pltpu.make_async_copy(pin_h, pin, p_sem.at[0]), pltpu.make_async_copy(pout_h, pout, p_sem.at[1])]

    def load(h, w):
        q = pl.ds(first(h), homes)
        return pltpu.make_async_copy((acts_h, grads_h)[w].at[q], (acts, grads)[w].at[q], in_sem.at[h, w])

    for w in range(2):
        loads[w].start()
        when_some(target(0), lambda: load(target(0), w).start())

    barrier = pltpu.get_barrier_semaphore()

    def greet(*place):
        pl.semaphore_signal(barrier, inc=1, device_id=dev(*place), device_id_type=pl.DeviceIdType.MESH)

    for d in range(1, slices):
        greet(*at_spot(lax.rem(spot + d, slices), r))
    for d in range(1, rows):
        greet(g, lax.rem(r + d, rows), c, s)
    guests = slices - 1 + rows - 1

    def more(i):
        h = target(i + 1)
        when_some(h, lambda: [load(h, w).start() for w in range(2)])

    each(rows - 1, more)

    def gram_copy(n):
        i = (other if n % subs == 0 else s) * per + n // subs
        return pltpu.make_async_copy(
            gram_h.at[pl.ds(pl.multiple_of(i * mb, mb), mb), pl.ds(pl.multiple_of(g * kw, kw), kw)],
            gram.at[n], gram_sem.at[n])

    store_copy = pltpu.make_async_copy(store_h, store, store_sem.at[0])

    def relay_copy(w, q):
        return remote(send.at[w, q], relay.at[w, q], rs_send.at[w, q], rl_recv.at[w, q], g, partner, c, s)

    def home_copy(w, h, k):
        q = first(h) + k
        return remote(send.at[w, q], recv.at[pair, w, k], rs_send.at[w, q], rh_recv.at[pair, w, k], g, h, c, s)

    def project(i):
        h = target(i)

        def _():
            q = pl.ds(first(h), homes)
            for w, (x, y) in enumerate(((acts, pin), (grads, pout))):
                if isinstance(i, int) and i == 0:
                    loads[w].wait()
                load(h, w).wait()
                value = jnp.dot(x[q].reshape(homes * tokens, depth), y[...],
                                preferred_element_type=F32).reshape(homes, tokens, kin)
                part[w, q] = value
                if isinstance(i, int) and i == 0 and w == 0:
                    pl.semaphore_wait(barrier, guests)

                @pl.when(jnp.logical_not(jnp.logical_or(h == r, relays(h))))
                def _():
                    send[w, q] = encode(value, 4, ps)
                    for k in range(homes):
                        @pl.when(h == partner)
                        def _():
                            home_copy(w, h, k).start()

                        @pl.when(h != partner)
                        def _():
                            relay_copy(w, first(h) + k).start()

        when_some(h, _)

    if rows > 8:
        for l in loads:
            l.wait()
        pl.semaphore_wait(barrier, guests)
    each(rows, project)
    for n in range(blocks):
        gram_copy(n).start()
    store_copy.start()

    def forward(i):
        h = target(i)

        def _():
            @pl.when(relays(h))
            def _():
                for w in range(2):
                    for k in range(homes):
                        q = first(h) + k
                        relay_copy(w, q).wait_recv()
                        send[w, q] = encode(part[w, q] + decode(relay[w, q], 4, ps), 4, ps)
                        home_copy(w, h, k).start()

        @pl.when(h != partner)
        def _():
            when_some(h, _)

    each(rows - 1, forward)

    unit = first(r) // homes

    def fx_copy(z, row, o):
        return remote(fsend.at[z, o], fbuf.at[z, unit, source], fx_send.at[z, row, o], fx_recv.at[z, unit],
                      *at_spot(o, row))

    def fx_own(z):
        return pltpu.make_async_copy(fsend.at[z, spot], fbuf.at[z, unit, source], fx_recv.at[z, unit])

    def users(z, use):
        def slice_of(d):
            o = lax.rem(spot + d + 1, slices)

            def row_of(j):
                row = jnp.where(2 * r < rows, rows - 1 - j, j)
                if isinstance(d, int) and d < slices - 1:
                    use(fx_copy(z, row, o))
                else:
                    @pl.when(jnp.logical_or(row != r, o != spot))
                    def _():
                        use(fx_copy(z, row, o))

            each(rows, row_of)

        each(slices, slice_of)

    def final():
        for k in range(homes):
            q = first(r) + k
            sides = []
            for w in range(2):
                value = part[w, q]
                for o in range(rows // 2):
                    remote(send.at[w, q], recv.at[o, w, k], rs_send.at[w, q], rh_recv.at[o, w, k],
                           g, partner, c, s).wait_recv()
                    value = value + decode(recv[o, w, k], 4, ps)
                sides.append(value)
            ah, al = split(sides[0].T)
            gh, gl = split(sides[1])
            f = jnp.dot(jnp.concatenate([ah, al, ah], axis=1), jnp.concatenate([gh, gh, gl], axis=0),
                        preferred_element_type=F32)
            f = f.reshape(slices, aw, kout)
            for z in range(parts):
                fsend[z, :, k] = encode(f[:, z * az:(z + 1) * az], 3, fs)
        for z in range(parts):
            users(z, lambda copy: copy.start())
            fx_own(z).start()

    when_some(r, final)

    width = ft.shape[1]
    allq = groups * nq

    def take(z):
        for u in range(queries // homes):
            remote(fbuf.at[z, u], fbuf.at[z, u], fx_send.at[0, 0, 0], fx_recv.at[z, u], g, partner, c, s).wait_recv()
            for k in range(homes):
                feats[:, u * homes + k, z * az:(z + 1) * az] = decode(fbuf[z, u, :, k], 3, fs)
        for a in range(z * az, (z + 1) * az):
            x = feats[:, :, a, :].reshape(allq, kout)
            xh, xl = split(x)
            rest = [jnp.zeros((width - 2 * allq, kout), F32)] if width > 2 * allq else []
            y = jnp.concatenate([xh.astype(F32), xl.astype(F32)] + rest, axis=0)
            ft[a * kout:(a + 1) * kout, :] = y.T.astype(BF16)

    def sub_copy(p):
        return remote(pre.at[p], sub_in.at[p], ps_send.at[p], ps_recv.at[p], g, r, c, other)

    spread = groups * cols
    mine = g * cols + c

    def v_copy(p, d):
        o = lax.rem(mine + d, spread)
        return remote(vsend.at[p, o // cols], vin.at[p, d], pv_send.at[p, d], pv_recv.at[p, d],
                      o // cols, r, lax.rem(o, cols), s)

    def product(n):
        acc = jnp.dot(gram[n, :, kw - kz:].astype(BF16), ft[kw - kz:], preferred_element_type=F32)
        if parts > 1:
            acc = acc + early[n]
        t = acc.T
        return t[:allq] + t[allq:2 * allq]

    def theirs(p):
        pre[p] = product(subs * p)
        sub_copy(p).start()

    def combine(p):
        sub_copy(p).wait_recv()
        value = (tot[p] + sub_in[p].reshape(groups, nq, mb))
        tot[p] = value
        vsend[p] = encode(value, 2, gs)
        for d in range(1, spread):
            v_copy(p, d).start()

    for n in range(blocks):
        gram_copy(n).wait()
    for z in range(parts):
        take(z)
        if z < parts - 1:
            for n in range(0, blocks, 2):
                acc = jnp.dot(gram[n:n + 2, :, z * kz:(z + 1) * kz].reshape(2 * mb, kz).astype(BF16),
                              ft[z * kz:(z + 1) * kz], preferred_element_type=F32).reshape(2, mb, width)
                early[n:n + 2] = acc + early[n:n + 2] if z else acc
    theirs(0)
    for p in range(per):
        if p + 1 < per:
            theirs(p + 1)
        tot[p] = product(subs * p + 1).reshape(groups, nq, mb)
        combine(p)
    store_copy.wait()
    score = None
    for p in range(per):
        value = tot[p, g]
        for d in range(1, spread):
            v_copy(p, d).wait_recv()
            value = value + decode(vin[p, d], 2, gs)
        term = lax.dot_general(jnp.concatenate(split(value), axis=0), store[:, p * mb:(p + 1) * mb],
                               (((1,), (1,)), ((), ())), preferred_element_type=F32)
        score = term if score is None else score + term
    score = score[:nq] + score[nq:]

    hq = nq // subs
    for o in range(subs):
        own[o] = score[o * hq:(o + 1) * hq]
    x_half = remote(own.at[other], half_in, ss_sem.at[0], ss_sem.at[1], g, r, c, other)
    x_half.start()
    x_half.wait()
    half = own[s] + half_in[...]
    own_s[...] = encode(half, 2, zs)
    x_rows = [remote(own_s, half_all.at[d], sz_send.at[d], sz_recv.at[d], g, lax.rem(r + d, rows), c, s)
              for d in range(1, rows)]
    for x in x_rows:
        x.start()
    half_in[...] = half
    for p in range(per):
        sub_copy(p).wait_send()
        for d in range(1, spread):
            v_copy(p, d).wait_send()
    for z in range(parts):
        when_some(r, lambda: users(z, lambda copy: copy.wait_send()))

    def drain(i):
        h = target(i)

        def _():
            for w in range(2):
                for k in range(homes):
                    relay_copy(w, first(h) + k).wait_send()

        when_some(h, _)

    each(rows - 1, drain)
    total = half_in[...]
    for d in range(1, rows):
        x_rows[d - 1].wait()
        total = total + decode(half_all[d], 2, zs)
    half_out[s] = total
    x_out = remote(half_out.at[s], half_out.at[s], sf_sem.at[0], sf_sem.at[1], g, r, c, other)
    x_out.start()
    x_out.wait()
    for o in range(subs):
        out[o * hq:(o + 1) * hq, :] = half_out[o]


def body(sizes, query_acts, query_grads, proj_in, proj_out, inverse_gram, store_slab):
    groups, rows, cols, subs = sizes
    queries, tokens, depth = query_acts.shape
    kin, kout = proj_in.shape[1], proj_out.shape[1]
    planes = cols * subs
    slices = groups * planes
    nq = planes * queries
    aw = kin // slices
    grows, gcols = inverse_gram.shape
    kw = gcols // groups
    mb = min(512, grows // subs)
    blocks = grows // mb
    per = blocks // subs
    spread = groups * cols
    examples = store_slab.shape[0]
    hq = nq // subs
    homes = -(-queries // rows)
    assert rows % 2 == 0 and subs == 2 and (queries % rows == 0 or rows % queries == 0)
    dma = pltpu.SemaphoreType.DMA
    lanes = -(-2 * groups * nq // 128) * 128
    parts = 2 if aw % 16 == 0 else 1
    scratch = [
        pltpu.VMEM(query_acts.shape, BF16), pltpu.VMEM(query_grads.shape, BF16),
        pltpu.VMEM(proj_in.shape, BF16), pltpu.VMEM(proj_out.shape, BF16),
        pltpu.VMEM((blocks, mb, kw), F32), pltpu.VMEM(store_slab.shape, BF16),
        pltpu.VMEM((2, queries, tokens, kin), F32), pltpu.VMEM((2, queries, tokens, kin), BF16),
        pltpu.VMEM((2, queries, tokens, kin), BF16), pltpu.VMEM((rows // 2, 2, homes, tokens, kin), BF16),
        pltpu.VMEM((parts, slices, homes, aw // parts, kout), BF16),
        pltpu.VMEM((parts, queries // homes, slices, homes, aw // parts, kout), BF16),
        pltpu.VMEM((slices, queries, aw, kout), F32), pltpu.VMEM((kw, lanes), BF16),
        pltpu.VMEM((blocks, mb, lanes) if parts > 1 else (1, 8, 128), F32),
        pltpu.VMEM((per, groups * nq, mb), F32), pltpu.VMEM((per, groups * nq, mb), F32),
        pltpu.VMEM((per, groups, nq, mb), F32),
        pltpu.VMEM((per, groups, nq, mb), BF16), pltpu.VMEM((per, spread, nq, mb), BF16),
        pltpu.VMEM((subs, hq, examples), F32), pltpu.VMEM((hq, examples), BF16), pltpu.VMEM((hq, examples), F32),
        pltpu.VMEM((rows, hq, examples), BF16), pltpu.VMEM((subs, hq, examples), F32),
        dma((2,)), dma((rows, 2)), dma((blocks,)), dma((1,)), dma((2, queries)), dma((2, queries)),
        dma((rows // 2, 2, homes)), dma((parts, rows, slices)), dma((parts, queries // homes)),
        dma((per,)), dma((per,)), dma((per, spread)), dma((per, spread)),
        dma((2,)), dma((rows,)), dma((rows,)), dma((2,)),
    ]
    return pl.pallas_call(
        functools.partial(kernel, groups, rows, cols, subs),
        out_shape=jax.ShapeDtypeStruct((nq, examples), F32),
        in_specs=[pl.BlockSpec(memory_space=pltpu.HBM)] * 6,
        out_specs=pl.BlockSpec(memory_space=pltpu.VMEM),
        scratch_shapes=scratch,
        compiler_params=pltpu.CompilerParams(
            collective_id=0, has_side_effects=True, vmem_limit_bytes=50 << 20),
        name="influence",
    )(*(pltpu.with_memory_space_constraint(a, pltpu.HBM) for a in (query_acts, query_grads, proj_in, proj_out, inverse_gram, store_slab)))


def solution(mesh):
    sizes = tuple(mesh.shape[n] for n in ("groups", "row", "col", "sub"))
    return jax.shard_map(
        functools.partial(body, sizes),
        mesh=mesh,
        in_specs=(
            P(("groups", "col", "sub"), None, "row"),
            P(("groups", "col", "sub"), None, "row"),
            P("row", None),
            P("row", None),
            P("row", ("col", "sub")),
            P(("groups", "col"), ("row", "sub")),
        ),
        out_specs=P("groups", "col"),
        check_vma=False,
    )
```

```python
import functools
import math

import jax
import jax.numpy as jnp
from jax import lax
from jax.experimental import pallas as pl
from jax.experimental.pallas import tpu as pltpu
from jax.sharding import PartitionSpec as P

F32, BF16 = jnp.float32, jnp.bfloat16
ACT_MAX, GRAD_MAX, PROJ_MAX, GRAM_MAX, STORE_MAX = 6.0, 0.5390625, 0.09375, 2.01, 0.046875


def split(x):
    hi = x.astype(BF16)
    return hi, (x - hi.astype(F32)).astype(BF16)


def scale_of(p, bound):
    return 2.0 ** math.floor(126 / p - math.log2(bound))


def encode(x, p, scale):
    z = x * scale
    if p == 2:
        y = z * jnp.abs(z)
    elif p == 3:
        y = z * z * z
    else:
        y = (z * z) * (z * jnp.abs(z))
    return y.astype(BF16)


def decode(y, p, scale):
    y = y.astype(F32)
    m = jnp.abs(y)
    if p == 2:
        v = m * lax.rsqrt(m) * (1.0 / scale)
    elif p == 3:
        v = jnp.exp2(jnp.log2(m) * (1.0 / 3.0)) * (1.0 / scale)
    else:
        v = lax.rsqrt(lax.rsqrt(m)) * (1.0 / scale)
    return jnp.where(y > 0, v, jnp.where(y < 0, -v, 0.0))


def each(n, fn):
    if n <= 8:
        for i in range(n):
            fn(i)
    else:
        def step(i, _):
            fn(i)
            return 0
        lax.fori_loop(0, n, step, 0)


def kernel(groups, rows, cols, subs, acts_h, grads_h, pin_h, pout_h, gram_h, store_h, out,
           acts, grads, pin, pout, gram, store, part, send, relay, recv, fsend, fbuf, feats, ft, early,
           pre, sub_in, tot, vsend, vin, own, own_s, half_in, half_all,
           p_sem, in_sem, gram_sem, store_sem, rs_send, rl_recv, rh_recv, fx_send, fx_recv,
           ps_send, ps_recv, pv_send, pv_recv, ss_sem, sz_send, sz_recv):
    g, r, c, s = (lax.axis_index(n) for n in ("groups", "row", "col", "sub"))
    queries, tokens, depth = acts.shape
    planes = cols * subs
    slices = groups * planes
    me = c * subs + s
    spot = me * groups + g
    source = g * planes + me
    aw, kout = feats.shape[2], feats.shape[3]
    kin = pin.shape[1]
    blocks, mb, kw = gram.shape
    per = blocks // subs
    other = lax.rem(s + 1, subs)
    nq = planes * queries
    parts, _, homes, az, _ = fsend.shape
    kz = kw // parts
    act_bound = rows * depth * ACT_MAX * PROJ_MAX
    grad_bound = rows * depth * GRAD_MAX * PROJ_MAX
    feat_bound = tokens * act_bound * grad_bound
    ps = scale_of(4, max(act_bound, grad_bound))
    fs = scale_of(3, feat_bound)
    pre_bound = feat_bound * GRAM_MAX * gram_h.shape[1] * planes
    gs = scale_of(2, pre_bound)
    zs = scale_of(2, pre_bound * STORE_MAX * gram_h.shape[1] * planes)

    def dev(group, row, col, sub):
        return {"groups": group, "row": row, "col": col, "sub": sub}

    def remote(src, dst, snd, rcv, group, row, col, sub):
        return pltpu.make_async_remote_copy(
            src_ref=src, dst_ref=dst, send_sem=snd, recv_sem=rcv,
            device_id=dev(group, row, col, sub), device_id_type=pl.DeviceIdType.MESH)

    def at_spot(o, row):
        plane = o // groups
        return lax.rem(o, groups), row, plane // subs, lax.rem(plane, subs)

    def first(row):
        return (row * queries + rows - 1) // rows

    def when_some(h, fn):
        def run():
            fn()

        if queries % rows == 0:
            run()
        else:
            pl.when(first(h) < first(h + 1))(run)

    odd = lax.rem(r, 2)
    pair = r // 2
    partner = r + 1 - 2 * odd

    def target(i):
        h = jnp.where(odd == 1, jnp.where(i < r, i, rows - 1 - i + r),
                      jnp.where(i < rows - 1 - r, rows - 1 - i, i - (rows - 1 - r)))
        return jnp.where(i == rows - 1, r, h)

    def relays(h):
        return jnp.where(odd == 1, h > r, h < r)

    loads = [pltpu.make_async_copy(pin_h, pin, p_sem.at[0]), pltpu.make_async_copy(pout_h, pout, p_sem.at[1])]

    def load(h, w):
        q = pl.ds(first(h), homes)
        return pltpu.make_async_copy((acts_h, grads_h)[w].at[q], (acts, grads)[w].at[q], in_sem.at[h, w])

    for w in range(2):
        loads[w].start()
        when_some(target(0), lambda: load(target(0), w).start())

    barrier = pltpu.get_barrier_semaphore()

    def greet(*place):
        pl.semaphore_signal(barrier, inc=1, device_id=dev(*place), device_id_type=pl.DeviceIdType.MESH)

    for d in range(1, slices):
        greet(*at_spot(lax.rem(spot + d, slices), r))
    for d in range(1, rows):
        greet(g, lax.rem(r + d, rows), c, s)
    guests = slices - 1 + rows - 1

    def more(i):
        h = target(i + 1)
        when_some(h, lambda: [load(h, w).start() for w in range(2)])

    each(rows - 1, more)

    def gram_copy(n):
        i = (other if n % subs == 0 else s) * per + n // subs
        return pltpu.make_async_copy(
            gram_h.at[pl.ds(pl.multiple_of(i * mb, mb), mb), pl.ds(pl.multiple_of(g * kw, kw), kw)],
            gram.at[n], gram_sem.at[n])

    store_copy = pltpu.make_async_copy(store_h, store, store_sem.at[0])

    def relay_copy(w, q):
        return remote(send.at[w, q], relay.at[w, q], rs_send.at[w, q], rl_recv.at[w, q], g, partner, c, s)

    def home_copy(w, h, k):
        q = first(h) + k
        return remote(send.at[w, q], recv.at[pair, w, k], rs_send.at[w, q], rh_recv.at[pair, w, k], g, h, c, s)

    def project(i):
        h = target(i)

        def _():
            q = pl.ds(first(h), homes)
            for w, (x, y) in enumerate(((acts, pin), (grads, pout))):
                if isinstance(i, int) and i == 0:
                    loads[w].wait()
                load(h, w).wait()
                value = jnp.dot(x[q].reshape(homes * tokens, depth), y[...],
                                preferred_element_type=F32).reshape(homes, tokens, kin)
                part[w, q] = value
                if isinstance(i, int) and i == 0 and w == 0:
                    pl.semaphore_wait(barrier, guests)

                @pl.when(jnp.logical_not(jnp.logical_or(h == r, relays(h))))
                def _():
                    send[w, q] = encode(value, 4, ps)
                    for k in range(homes):
                        @pl.when(h == partner)
                        def _():
                            home_copy(w, h, k).start()

                        @pl.when(h != partner)
                        def _():
                            relay_copy(w, first(h) + k).start()

        when_some(h, _)

    if rows > 8:
        for l in loads:
            l.wait()
        pl.semaphore_wait(barrier, guests)
    each(rows, project)
    for n in range(blocks):
        gram_copy(n).start()
    store_copy.start()

    def forward(i):
        h = target(i)

        def _():
            @pl.when(relays(h))
            def _():
                for w in range(2):
                    for k in range(homes):
                        q = first(h) + k
                        relay_copy(w, q).wait_recv()
                        send[w, q] = encode(part[w, q] + decode(relay[w, q], 4, ps), 4, ps)
                        home_copy(w, h, k).start()

        @pl.when(h != partner)
        def _():
            when_some(h, _)

    each(rows - 1, forward)

    unit = first(r) // homes

    def fx_copy(z, row, o):
        return remote(fsend.at[z, o], fbuf.at[z, unit, source], fx_send.at[z, row, o], fx_recv.at[z, unit],
                      *at_spot(o, row))

    def fx_own(z):
        return pltpu.make_async_copy(fsend.at[z, spot], fbuf.at[z, unit, source], fx_recv.at[z, unit])

    def users(z, use):
        def slice_of(d):
            o = lax.rem(spot + d + 1, slices)

            def row_of(j):
                row = jnp.where(2 * r < rows, rows - 1 - j, j)
                if isinstance(d, int) and d < slices - 1:
                    use(fx_copy(z, row, o))
                else:
                    @pl.when(jnp.logical_or(row != r, o != spot))
                    def _():
                        use(fx_copy(z, row, o))

            each(rows, row_of)

        each(slices, slice_of)

    def final():
        for k in range(homes):
            q = first(r) + k
            sides = []
            for w in range(2):
                value = part[w, q]
                for o in range(rows // 2):
                    remote(send.at[w, q], recv.at[o, w, k], rs_send.at[w, q], rh_recv.at[o, w, k],
                           g, partner, c, s).wait_recv()
                    value = value + decode(recv[o, w, k], 4, ps)
                sides.append(value)
            ah, al = split(sides[0].T)
            gh, gl = split(sides[1])
            f = jnp.dot(jnp.concatenate([ah, al, ah], axis=1), jnp.concatenate([gh, gh, gl], axis=0),
                        preferred_element_type=F32)
            f = f.reshape(slices, aw, kout)
            for z in range(parts):
                fsend[z, :, k] = encode(f[:, z * az:(z + 1) * az], 3, fs)
        for z in range(parts):
            users(z, lambda copy: copy.start())
            fx_own(z).start()

    when_some(r, final)

    width = ft.shape[1]
    allq = groups * nq

    def take(z):
        for u in range(queries // homes):
            remote(fbuf.at[z, u], fbuf.at[z, u], fx_send.at[0, 0, 0], fx_recv.at[z, u], g, partner, c, s).wait_recv()
            for k in range(homes):
                feats[:, u * homes + k, z * az:(z + 1) * az] = decode(fbuf[z, u, :, k], 3, fs)
        for a in range(z * az, (z + 1) * az):
            x = feats[:, :, a, :].reshape(allq, kout)
            xh, xl = split(x)
            rest = [jnp.zeros((width - 2 * allq, kout), F32)] if width > 2 * allq else []
            y = jnp.concatenate([xh.astype(F32), xl.astype(F32)] + rest, axis=0)
            ft[a * kout:(a + 1) * kout, :] = y.T.astype(BF16)

    def sub_copy(p):
        return remote(pre.at[p], sub_in.at[p], ps_send.at[p], ps_recv.at[p], g, r, c, other)

    spread = groups * cols
    mine = g * cols + c

    def v_copy(p, d):
        o = lax.rem(mine + d, spread)
        return remote(vsend.at[p, o // cols], vin.at[p, d], pv_send.at[p, d], pv_recv.at[p, d],
                      o // cols, r, lax.rem(o, cols), s)

    def product(n):
        acc = jnp.dot(gram[n, :, kw - kz:].astype(BF16), ft[kw - kz:], preferred_element_type=F32)
        if parts > 1:
            acc = acc + early[n]
        t = acc.T
        return t[:allq] + t[allq:2 * allq]

    def theirs(p):
        pre[p] = product(subs * p)
        sub_copy(p).start()

    def combine(p):
        sub_copy(p).wait_recv()
        value = (tot[p] + sub_in[p].reshape(groups, nq, mb))
        tot[p] = value
        vsend[p] = encode(value, 2, gs)
        for d in range(1, spread):
            v_copy(p, d).start()

    for n in range(blocks):
        gram_copy(n).wait()
    for z in range(parts):
        take(z)
        if z < parts - 1:
            for n in range(0, blocks, 2):
                acc = jnp.dot(gram[n:n + 2, :, z * kz:(z + 1) * kz].reshape(2 * mb, kz).astype(BF16),
                              ft[z * kz:(z + 1) * kz], preferred_element_type=F32).reshape(2, mb, width)
                early[n:n + 2] = acc + early[n:n + 2] if z else acc
    theirs(0)
    for p in range(per):
        if p + 1 < per:
            theirs(p + 1)
        tot[p] = product(subs * p + 1).reshape(groups, nq, mb)
        combine(p)
    store_copy.wait()
    score = None
    for p in range(per):
        value = tot[p, g]
        for d in range(1, spread):
            v_copy(p, d).wait_recv()
            value = value + decode(vin[p, d], 2, gs)
        term = lax.dot_general(jnp.concatenate(split(value), axis=0), store[:, p * mb:(p + 1) * mb],
                               (((1,), (1,)), ((), ())), preferred_element_type=F32)
        score = term if score is None else score + term
    score = score[:nq] + score[nq:]

    hq = nq // subs
    for o in range(subs):
        own[o] = score[o * hq:(o + 1) * hq]
    x_half = remote(own.at[other], half_in, ss_sem.at[0], ss_sem.at[1], g, r, c, other)
    x_half.start()
    x_half.wait()
    half = own[s] + half_in[...]
    own_s[...] = encode(half, 2, zs)
    ring = rows * subs
    x_rows = []
    for d in range(1, ring):
        o = lax.rem(r * subs + s + d, ring)
        x_rows.append(remote(own_s, half_all.at[d], sz_send.at[d], sz_recv.at[d], g, o // subs, c, lax.rem(o, subs)))
    for x in x_rows:
        x.start()
    half_in[...] = half
    for p in range(per):
        sub_copy(p).wait_send()
        for d in range(1, spread):
            v_copy(p, d).wait_send()
    for z in range(parts):
        when_some(r, lambda: users(z, lambda copy: copy.wait_send()))

    def drain(i):
        h = target(i)

        def _():
            for w in range(2):
                for k in range(homes):
                    relay_copy(w, first(h) + k).wait_send()

        when_some(h, _)

    each(rows - 1, drain)
    totals = [half_in[...], None]
    for d in range(1, ring):
        x_rows[d - 1].wait()
        part_d = decode(half_all[d], 2, zs)
        totals[d % subs] = part_d if totals[d % subs] is None else totals[d % subs] + part_d
    for o, total in zip((s, other), totals):
        out[pl.ds(pl.multiple_of(o * hq, hq), hq), :] = total


def body(sizes, query_acts, query_grads, proj_in, proj_out, inverse_gram, store_slab):
    groups, rows, cols, subs = sizes
    queries, tokens, depth = query_acts.shape
    kin, kout = proj_in.shape[1], proj_out.shape[1]
    planes = cols * subs
    slices = groups * planes
    nq = planes * queries
    aw = kin // slices
    grows, gcols = inverse_gram.shape
    kw = gcols // groups
    mb = min(512, grows // subs)
    blocks = grows // mb
    per = blocks // subs
    spread = groups * cols
    examples = store_slab.shape[0]
    hq = nq // subs
    homes = -(-queries // rows)
    assert rows % 2 == 0 and subs == 2 and (queries % rows == 0 or rows % queries == 0)
    dma = pltpu.SemaphoreType.DMA
    lanes = -(-2 * groups * nq // 128) * 128
    parts = 2 if aw % 16 == 0 else 1
    scratch = [
        pltpu.VMEM(query_acts.shape, BF16), pltpu.VMEM(query_grads.shape, BF16),
        pltpu.VMEM(proj_in.shape, BF16), pltpu.VMEM(proj_out.shape, BF16),
        pltpu.VMEM((blocks, mb, kw), F32), pltpu.VMEM(store_slab.shape, BF16),
        pltpu.VMEM((2, queries, tokens, kin), F32), pltpu.VMEM((2, queries, tokens, kin), BF16),
        pltpu.VMEM((2, queries, tokens, kin), BF16), pltpu.VMEM((rows // 2, 2, homes, tokens, kin), BF16),
        pltpu.VMEM((parts, slices, homes, aw // parts, kout), BF16),
        pltpu.VMEM((parts, queries // homes, slices, homes, aw // parts, kout), BF16),
        pltpu.VMEM((slices, queries, aw, kout), F32), pltpu.VMEM((kw, lanes), BF16),
        pltpu.VMEM((blocks, mb, lanes) if parts > 1 else (1, 8, 128), F32),
        pltpu.VMEM((per, groups * nq, mb), F32), pltpu.VMEM((per, groups * nq, mb), F32),
        pltpu.VMEM((per, groups, nq, mb), F32),
        pltpu.VMEM((per, groups, nq, mb), BF16), pltpu.VMEM((per, spread, nq, mb), BF16),
        pltpu.VMEM((subs, hq, examples), F32), pltpu.VMEM((hq, examples), BF16), pltpu.VMEM((hq, examples), F32),
        pltpu.VMEM((rows * subs, hq, examples), BF16),
        dma((2,)), dma((rows, 2)), dma((blocks,)), dma((1,)), dma((2, queries)), dma((2, queries)),
        dma((rows // 2, 2, homes)), dma((parts, rows, slices)), dma((parts, queries // homes)),
        dma((per,)), dma((per,)), dma((per, spread)), dma((per, spread)),
        dma((2,)), dma((rows * subs,)), dma((rows * subs,)),
    ]
    return pl.pallas_call(
        functools.partial(kernel, groups, rows, cols, subs),
        out_shape=jax.ShapeDtypeStruct((nq, examples), F32),
        in_specs=[pl.BlockSpec(memory_space=pltpu.HBM)] * 6,
        out_specs=pl.BlockSpec(memory_space=pltpu.VMEM),
        scratch_shapes=scratch,
        compiler_params=pltpu.CompilerParams(
            collective_id=0, has_side_effects=True, vmem_limit_bytes=50 << 20),
        name="influence",
    )(*(pltpu.with_memory_space_constraint(a, pltpu.HBM) for a in (query_acts, query_grads, proj_in, proj_out, inverse_gram, store_slab)))


def solution(mesh):
    sizes = tuple(mesh.shape[n] for n in ("groups", "row", "col", "sub"))
    return jax.shard_map(
        functools.partial(body, sizes),
        mesh=mesh,
        in_specs=(
            P(("groups", "col", "sub"), None, "row"),
            P(("groups", "col", "sub"), None, "row"),
            P("row", None),
            P("row", None),
            P("row", ("col", "sub")),
            P(("groups", "col"), ("row", "sub")),
        ),
        out_specs=P("groups", "col"),
        check_vma=False,
    )
```
